32 devices in a mesh: row: 8 (over y, x, core), col: 4 (over z).
Axes of the slice: x: 2, y: 2, z: 4, core: 2. Of those that a mesh axis runs over, the one named last changes fastest.
Arguments:
- inverse: float32 [20480, 20480], P('row', 'col'), may hold values from -6 to 6
- factor: float32 [20480, 2, 256], P(('row', 'col')), may hold values from -0.0390625 to 0.0390625
- diag_inverse: float32 [2, 256, 256], replicated, may hold values from -6 to 6
- block_sizes: int32 [64], replicated, may hold values from 1 to 1280, 20480 in all
- listed: int32 [2, 64], replicated, may hold values 0 or 1
Outputs:
- ancestor_rows: float32 [20480, 2, 256], P(('row', 'col'))
- diagonal_block: float32 [2, 256, 256], replicated
The draws below stay inside these ranges and needn't reach their ends.
Inputs may be any that keep to these rules, and one draw needn't show every extreme that they name: `block_sizes`: positive sizes that sum to 20480; the largest is exactly 1280.
All inputs are finite; a program needn't handle non-finite values.
Results may differ from the reference program's by a relative error of at most 0.00007.
Values sent between devices are 32-bit elements; how exact they have to be, the bound alone decides.
A program may use at most 128 MiB of HBM per device.

```python
import math
import jax
import jax.numpy as jnp
import numpy as np
from jax import lax

NA = 20480
W = 256
SIBS = 2
NBLK = 64
MOSTB = 1280


def place_ends(array, own_key, smallest, top_value):
    longest = array.shape.index(max(array.shape))
    spots = []
    for shift in (0, 1):
        where = [jax.random.randint(jax.random.fold_in(own_key, axis), (), 0, length) for axis, length in enumerate(array.shape)]
        where[longest] = (where[longest] + shift) % array.shape[longest]
        spots.append(tuple(where))
    return array.at[spots[0]].set(smallest).at[spots[1]].set(top_value)


def steps_of(key, extent, cuts, smallest, largest):
    def one(axis_at, shards_of):
        draws = jax.random.uniform(jax.random.fold_in(jax.random.fold_in(key, 6), axis_at), (shards_of,), jnp.float32, smallest / len(cuts), largest / len(cuts))
        return jnp.repeat(jnp.exp(draws), extent[axis_at] // shards_of).reshape((-1,) + (1,) * (len(extent) - axis_at - 1))

    level = one(*cuts[0])
    for cut in cuts[1:]:
        level = level * one(*cut)
    return level


def profile(count, total, reach, lean):
    weights = [(1 << 20) // math.isqrt(rank ** lean) + 1 for rank in range(2, count + 1)]
    rest, given = total - reach - (count - 1), [1] * (count - 1)
    while rest > 0:
        movable = [i for i in range(count - 1) if given[i] < reach]
        pool, left = sum([weights[i] for i in movable]), rest
        for i in movable:
            addition = min(reach - given[i], max(1, left * weights[i] // pool), rest)
            given[i] = given[i] + addition
            rest = rest - addition
    return np.array([reach] + given)


def uneven(key, count, total, limit, slope):
    if count == 2:
        one = jax.random.randint(key, (), max(1, total - limit), min(limit, total - 1) + 1)
        return jnp.stack([one, total - one])
    tallies = jnp.asarray(profile(count, total, limit, slope), jnp.int32)
    pairs = (count - 1) // 2
    donor, taker = tallies[1:1 + 2 * pairs:2], tallies[2:2 + 2 * pairs:2]
    room = jnp.minimum(donor - 1, limit - taker)
    passed = jax.random.randint(jax.random.fold_in(key, 1), (pairs,), 0, 1 << 20) % (room + 1)
    tallies = tallies.at[1:1 + 2 * pairs:2].set(donor - passed).at[2:2 + 2 * pairs:2].set(taker + passed)
    return tallies[jax.random.permutation(jax.random.fold_in(key, 2), count)]


def scatter_about(rng, dims, deviation, bound, shards=(), held_as=jnp.bfloat16):
    factor_of = steps_of(rng, dims, shards, -0.22, 0.18) if shards else 1.0
    result = jax.random.normal(rng, dims, jnp.float32) * deviation * factor_of
    return jnp.minimum(jnp.maximum(result, -bound), bound).astype(held_as)


def setup_inputs(seed: int = 0) -> dict:
    key_of = jax.random.split(jax.random.key(seed), 6)
    return {
        "inverse": scatter_about(key_of[0], (NA, NA), 1.0, 6.0, ((0, 8), (1, 4)), jnp.float32),
        "factor": scatter_about(key_of[1], (NA, SIBS, W), NA ** -0.5, 0.0390625, ((0, 32),), jnp.float32),
        "diag_inverse": scatter_about(key_of[2], (SIBS, W, W), 1.0, 6.0, (), jnp.float32),
        "block_sizes": uneven(key_of[3], NBLK, NA, MOSTB, 2).astype(jnp.int32),
        "listed": place_ends((jax.random.randint(key_of[4], (SIBS, NBLK), 0, 2) < 1).astype(jnp.int32), jax.random.fold_in(key_of[4], 1), 0, 1),
    }


def membership(first_row, row_total, block_sizes, listed):
    block_ends = jnp.cumsum(block_sizes).astype(jnp.int32)
    block_starts = block_ends - block_sizes.astype(jnp.int32)
    positions = first_row + jnp.arange(row_total, dtype=jnp.int32)
    inside = ((positions[:, None] >= block_starts[None, :]) & (positions[:, None] < block_ends[None, :])).astype(jnp.float32)
    return jnp.dot(inside, listed.astype(jnp.float32).T, precision=lax.Precision.HIGHEST, preferred_element_type=jnp.float32)


def reference(inverse, factor, diag_inverse, block_sizes, listed):
    member = membership(0, NA, block_sizes, listed)
    masked = factor * member[:, :, None]
    panel = masked.reshape(NA, SIBS * W)
    product = -jnp.dot(inverse, panel, precision=lax.Precision.HIGHEST, preferred_element_type=jnp.float32)
    ancestor_rows = product.reshape(NA, SIBS, W) * member[:, :, None]
    schur = jnp.einsum("isw,isv->swv", factor, ancestor_rows, precision=lax.Precision.HIGHEST)
    return ancestor_rows, diag_inverse - schur
```

```python
import functools
import math

import jax
import jax.numpy as jnp
from jax import lax
from jax.experimental import pallas as pl
from jax.experimental.pallas import tpu as pltpu
from jax.sharding import PartitionSpec as P

MESH = pl.DeviceIdType.MESH


def membership(first_row, row_total, block_sizes, listed):
    block_ends = jnp.cumsum(block_sizes)
    block_starts = block_ends - block_sizes
    positions = first_row + jnp.arange(row_total, dtype=jnp.int32)
    inside = (
        (positions[:, None] >= block_starts[None, :]) & (positions[:, None] < block_ends[None, :])
    ).astype(jnp.float32)
    return jnp.dot(
        inside,
        listed.astype(jnp.float32).T,
        precision=lax.Precision.HIGHEST,
        preferred_element_type=jnp.float32,
    )


def holder(k, n_rowdev, n_coldev):
    ratio = n_rowdev // n_coldev
    part = k // n_coldev
    place = k % n_coldev
    return (place + (part % 2) * (n_coldev - 1 - 2 * place)) * ratio + part


def shard_of(row, n_rowdev, n_coldev):
    ratio = n_rowdev // n_coldev
    part = row % ratio
    place = row // ratio
    return part * n_coldev + place + (part % 2) * (n_coldev - 1 - 2 * place)


def flip(row, bit):
    return row + bit * (1 - 2 * ((row // bit) % 2))


def product_kernel(
    n_rowdev, n_coldev, parts, depth,
    own_ref, inverse_ref, out_ref,
    panel, high, low, tiles, sums, from_below, from_above,
    gather_send, gather_recv, tile_sem, sum_send, below_recv, above_recv,
):
    row = lax.axis_index("row")
    col = lax.axis_index("col")
    sibling_count, shard_rows, width = own_ref.shape
    col_rows = panel.shape[1]
    piece = shard_rows // parts
    bits = [1 << i for i in range(n_rowdev.bit_length() - 1)]

    number = row * n_coldev + col
    target_row = holder(number % n_rowdev, n_rowdev, n_coldev)
    target_col = number // n_rowdev
    source = col * n_rowdev + shard_of(row, n_rowdev, n_coldev)
    source_row = source // n_coldev
    source_col = source % n_coldev
    moving = target_row * n_coldev + target_col != number

    barrier = pltpu.get_barrier_semaphore()

    def greet(to_row, to_col):
        pl.semaphore_signal(barrier, inc=1, device_id=(to_row, to_col), device_id_type=MESH)

    for bit in bits:
        greet(flip(row, bit), col)

    @pl.when(moving)
    def _():
        greet(target_row, target_col)
        greet(source_row, source_col)

    @pl.when(col > 0)
    def _():
        greet(row, col - 1)

    @pl.when(col < n_coldev - 1)
    def _():
        greet(row, col + 1)

    pl.semaphore_wait(
        barrier,
        len(bits)
        + jnp.where(moving, 2, 0)
        + jnp.where(col > 0, 1, 0)
        + jnp.where(col < n_coldev - 1, 1, 0),
    )

    def place(of_row, part):
        start = shard_of(of_row, n_rowdev, n_coldev) * shard_rows + part * piece
        return pl.ds(pl.multiple_of(start, 8), piece)

    def orders(s):
        rest = bits[1:]
        return (rest if s % 2 else rest[::-1]) + bits[:1]

    def move(s, part):
        return pltpu.make_async_remote_copy(
            src_ref=own_ref.at[s, pl.ds(part * piece, piece)],
            dst_ref=panel.at[s, place(target_row, part)],
            send_sem=gather_send.at[s, part, 0],
            recv_sem=gather_recv.at[s, part, 0],
            device_id=(target_row, target_col),
            device_id_type=MESH,
        )

    def keep(s, part):
        return pltpu.make_async_copy(
            own_ref.at[s, pl.ds(part * piece, piece)],
            panel.at[s, place(row, part)],
            gather_recv.at[s, part, 0],
        )

    def exchanges(s, part, stage):
        order = orders(s)
        held = [row]
        for bit in order[:stage - 1]:
            held = held + [flip(r, bit) for r in held]
        partner = flip(row, order[stage - 1])
        copies = []
        for m, slot in enumerate(held):
            entry = (1 << (stage - 1)) + m
            where = panel.at[s, place(slot, part)]
            copies.append(pltpu.make_async_remote_copy(
                src_ref=where,
                dst_ref=where,
                send_sem=gather_send.at[s, part, entry],
                recv_sem=gather_recv.at[s, part, entry],
                device_id=(partner, col),
                device_id_type=MESH,
            ))
        return copies

    def start_stage(s, part, stage):
        if stage == 0:
            @pl.when(moving)
            def _():
                move(s, part).start()

            @pl.when(jnp.logical_not(moving))
            def _():
                keep(s, part).start()
        else:
            for copy in exchanges(s, part, stage):
                copy.start()

    def end_stage(s, part, stage):
        if stage == 0:
            @pl.when(moving)
            def _():
                move(s, part).wait_recv()

            @pl.when(jnp.logical_not(moving))
            def _():
                keep(s, part).wait()
        else:
            for copy in exchanges(s, part, stage):
                copy.wait_recv()

    items = [(s, part) for part in range(parts) for s in range(sibling_count)]
    for s, part in items:
        start_stage(s, part, 0)

    others = (n_coldev - 1) * parts
    total = n_coldev * parts
    swap = col > n_coldev - 1 - col
    near = jnp.where(swap, n_coldev - 1 - col, col)
    lead = n_coldev - 1 - 2 * near
    minor_total = near * parts

    def plan(t):
        inner = t - lead
        paired = jnp.logical_and(inner >= 0, inner < 2 * minor_total)
        minor = jnp.logical_and(paired, inner % 2 == 1)
        major_at = jnp.where(inner < 0, t, jnp.where(paired, lead + inner // 2, t - minor_total))
        index = jnp.where(minor, inner // 2, major_at)
        up = jnp.where(swap, minor, jnp.logical_not(minor))
        block = jnp.where(up, n_coldev - 1 - index // parts, index // parts)
        is_own = t >= others
        block = jnp.where(is_own, col, block)
        part = jnp.where(is_own, t - others, index % parts)
        up = jnp.logical_and(up, jnp.logical_not(is_own))
        down = jnp.logical_and(jnp.logical_not(up), jnp.logical_not(is_own))
        return block, part, up, down, is_own

    def load(t):
        block, part, _, _, _ = plan(t)
        start = pl.multiple_of(block * shard_rows + part * piece, 8)
        return pltpu.make_async_copy(
            inverse_ref.at[pl.ds(start, piece)], tiles.at[t % 2], tile_sem.at[t % 2]
        )

    load(0).start()

    stages = 1 + len(bits)
    for tick in range(parts + stages):
        for s, part in items:
            stage = tick - part
            if 0 <= stage < stages:
                end_stage(s, part, stage)
                if stage + 1 < stages:
                    start_stage(s, part, stage + 1)

    @pl.loop(0, col_rows // 256 if col_rows % 256 == 0 else 1)
    def _(i):
        step = 256 if col_rows % 256 == 0 else col_rows
        rows = pl.ds(pl.multiple_of(i * step, step), step)
        for s in range(sibling_count):
            value = panel[s, rows, :]
            top = value.astype(jnp.bfloat16)
            high[rows, s * width:(s + 1) * width] = top
            low[rows, s * width:(s + 1) * width] = (
                value - top.astype(jnp.float32)
            ).astype(jnp.bfloat16)

    def pass_up(block, part):
        return pltpu.make_async_remote_copy(
            src_ref=sums.at[block, part],
            dst_ref=from_below.at[block, part],
            send_sem=sum_send.at[block, part],
            recv_sem=below_recv.at[block, part],
            device_id=(row, col + 1),
            device_id_type=MESH,
        )

    def pass_down(block, part):
        return pltpu.make_async_remote_copy(
            src_ref=sums.at[block, part],
            dst_ref=from_above.at[block, part],
            send_sem=sum_send.at[block, part],
            recv_sem=above_recv.at[block, part],
            device_id=(row, col - 1),
            device_id_type=MESH,
        )

    @pl.loop(0, total)
    def _(t):
        block, part, up, down, is_own = plan(t)

        @pl.when(t + 1 < total)
        def _():
            load(t + 1).start()

        load(t).wait()
        sums[block, part] = jnp.zeros((piece, sibling_count * width), jnp.float32)

        @pl.loop(0, col_rows // depth)
        def _(k):
            span = pl.ds(pl.multiple_of(k * depth, depth), depth)
            value = tiles[t % 2, :, span]
            top = value.astype(jnp.bfloat16)
            rest = (value - top.astype(jnp.float32)).astype(jnp.bfloat16)
            dot = functools.partial(jnp.dot, preferred_element_type=jnp.float32)
            sums[block, part] += (
                dot(top, low[span, :]) + dot(rest, high[span, :]) + dot(top, high[span, :])
            )

        @pl.when(jnp.logical_and(jnp.logical_not(down), col > 0))
        def _():
            pass_up(block, part).wait_recv()
            sums[block, part] += from_below[block, part]

        @pl.when(jnp.logical_and(jnp.logical_not(up), col < n_coldev - 1))
        def _():
            pass_down(block, part).wait_recv()
            sums[block, part] += from_above[block, part]

        @pl.when(up)
        def _():
            pass_up(block, part).start()

        @pl.when(down)
        def _():
            pass_down(block, part).start()

        @pl.when(is_own)
        def _():
            out_ref[part] = sums[block, part]

    @pl.loop(0, others)
    def _(t):
        block, part, up, down, _ = plan(t)

        @pl.when(up)
        def _():
            pass_up(block, part).wait_send()

        @pl.when(down)
        def _():
            pass_down(block, part).wait_send()

    for s, part in items:
        @pl.when(moving)
        def _():
            move(s, part).wait_send()

        for stage in range(1, stages):
            for copy in exchanges(s, part, stage):
                copy.wait_send()


def product(n_rowdev, n_coldev, inverse, own):
    sibling_count, shard_rows, width = own.shape
    block_total, col_rows = inverse.shape
    parts = 2 if shard_rows % 16 == 0 else 1
    piece = shard_rows // parts
    depth = math.gcd(col_rows, 1280)
    columns = sibling_count * width
    f32 = jnp.float32
    vmem = pl.BlockSpec(memory_space=pltpu.VMEM)
    out = pl.pallas_call(
        functools.partial(product_kernel, n_rowdev, n_coldev, parts, depth),
        out_shape=jax.ShapeDtypeStruct((parts, piece, columns), f32),
        in_specs=[vmem, pl.BlockSpec(memory_space=pl.ANY)],
        out_specs=vmem,
        scratch_shapes=[
            pltpu.VMEM((sibling_count, col_rows, width), f32),
            pltpu.VMEM((col_rows, columns), jnp.bfloat16),
            pltpu.VMEM((col_rows, columns), jnp.bfloat16),
            pltpu.VMEM((2, piece, col_rows), f32),
            pltpu.VMEM((n_coldev, parts, piece, columns), f32),
            pltpu.VMEM((n_coldev, parts, piece, columns), f32),
            pltpu.VMEM((n_coldev, parts, piece, columns), f32),
            pltpu.SemaphoreType.DMA((sibling_count, parts, n_rowdev)),
            pltpu.SemaphoreType.DMA((sibling_count, parts, n_rowdev)),
            pltpu.SemaphoreType.DMA((2,)),
            pltpu.SemaphoreType.DMA((n_coldev, parts)),
            pltpu.SemaphoreType.DMA((n_coldev, parts)),
            pltpu.SemaphoreType.DMA((n_coldev, parts)),
        ],
        compiler_params=pltpu.CompilerParams(
            collective_id=0, has_side_effects=True, vmem_limit_bytes=60_000_000
        ),
        name="gather_product_scatter",
    )(own, inverse)
    return out.reshape(shard_rows, columns)


def total_kernel(
    n_rowdev, n_coldev, x_ref, out_ref,
    got, mine, gathered, whole, first_send, first_recv, second_send, second_recv,
    third_send, third_recv,
):
    row = lax.axis_index("row")
    col = lax.axis_index("col")
    barrier = pltpu.get_barrier_semaphore()
    for step in range(1, n_rowdev):
        pl.semaphore_signal(
            barrier, inc=1, device_id=((row + step) % n_rowdev, col), device_id_type=MESH
        )
    for step in range(1, n_coldev):
        pl.semaphore_signal(
            barrier, inc=1, device_id=(row, (col + step) % n_coldev), device_id_type=MESH
        )
    pl.semaphore_wait(barrier, n_rowdev + n_coldev - 2)

    def scatter(step):
        peer = (row + step) % n_rowdev
        return pltpu.make_async_remote_copy(
            src_ref=x_ref.at[peer], dst_ref=got.at[step],
            send_sem=first_send.at[step], recv_sem=first_recv.at[step],
            device_id=(peer, col), device_id_type=MESH,
        )

    def share(step):
        return pltpu.make_async_remote_copy(
            src_ref=mine, dst_ref=gathered.at[step],
            send_sem=second_send.at[step], recv_sem=second_recv.at[step],
            device_id=(row, (col + step) % n_coldev), device_id_type=MESH,
        )

    def spread(step):
        return pltpu.make_async_remote_copy(
            src_ref=whole, dst_ref=out_ref.at[row],
            send_sem=third_send.at[step], recv_sem=third_recv.at[step],
            device_id=((row + step) % n_rowdev, col), device_id_type=MESH,
        )

    for step in range(1, n_rowdev):
        scatter(step).start()
    value = x_ref[row]
    for step in range(1, n_rowdev):
        scatter(step).wait_recv()
        value = value + got[step]
    mine[...] = value
    for step in range(1, n_coldev):
        share(step).start()
    for step in range(1, n_coldev):
        share(step).wait_recv()
    gathered[0] = mine[...]
    value = gathered[col]
    for place in range(1, n_coldev):
        value = value + gathered[(col - place + n_coldev) % n_coldev]
    whole[...] = value
    for step in range(1, n_rowdev):
        spread(step).start()
    out_ref[row] = whole[...]
    for step in range(1, n_rowdev):
        spread(step).wait_recv()
    for step in range(1, n_rowdev):
        scatter(step).wait_send()
        spread(step).wait_send()
    for step in range(1, n_coldev):
        share(step).wait_send()


def total(n_rowdev, n_coldev, value):
    rows, columns = value.shape
    piece = rows // n_rowdev
    vmem = pl.BlockSpec(memory_space=pltpu.VMEM)
    dma = pltpu.SemaphoreType.DMA
    out = pl.pallas_call(
        functools.partial(total_kernel, n_rowdev, n_coldev),
        out_shape=jax.ShapeDtypeStruct((n_rowdev, piece, columns), jnp.float32),
        in_specs=[vmem],
        out_specs=vmem,
        scratch_shapes=[
            pltpu.VMEM((n_rowdev, piece, columns), jnp.float32),
            pltpu.VMEM((piece, columns), jnp.float32),
            pltpu.VMEM((n_coldev, piece, columns), jnp.float32),
            pltpu.VMEM((piece, columns), jnp.float32),
            dma((n_rowdev,)), dma((n_rowdev,)), dma((n_coldev,)), dma((n_coldev,)),
            dma((n_rowdev,)), dma((n_rowdev,)),
        ],
        compiler_params=pltpu.CompilerParams(collective_id=1, has_side_effects=True),
        name="schur_total",
    )(value.reshape(n_rowdev, piece, columns))
    return out.reshape(rows, columns)


def per_device(inverse, factor, diag_inverse, block_sizes, listed):
    n_rowdev = lax.axis_size("row")
    n_coldev = lax.axis_size("col")
    row_place = lax.axis_index("row")
    col_place = lax.axis_index("col")
    shard_rows, sibling_count, width = factor.shape

    member = membership(
        (row_place * n_coldev + col_place) * shard_rows, shard_rows, block_sizes, listed
    )
    own = jnp.transpose(factor, (1, 0, 2))
    summed = product(n_rowdev, n_coldev, inverse, own * member.T[:, :, None])
    results = [
        -(summed[:, s * width:(s + 1) * width] * member[:, s:s + 1])
        for s in range(sibling_count)
    ]
    terms = [
        lax.dot_general(
            own[s], results[s], (((0,), (0,)), ((), ())),
            precision=lax.Precision.HIGHEST, preferred_element_type=jnp.float32,
        )
        for s in range(sibling_count)
    ]
    schur = total(n_rowdev, n_coldev, jnp.concatenate(terms, axis=0))
    schur = schur.reshape(sibling_count, width, width)
    ancestor_rows = jnp.stack(results, axis=1)
    return (ancestor_rows, diag_inverse - schur)


def solution(mesh):
    in_specs = (P("row", "col"), P(("row", "col"), None, None), P(), P(), P())
    out_specs = (P(("row", "col"), None, None), P())
    return jax.shard_map(
        per_device, mesh=mesh, in_specs=in_specs, out_specs=out_specs, check_vma=False
    )
```

```python
import functools
import math

import jax
import jax.numpy as jnp
from jax import lax
from jax.experimental import pallas as pl
from jax.experimental.pallas import tpu as pltpu
from jax.sharding import PartitionSpec as P

MESH = pl.DeviceIdType.MESH


def membership(first_row, row_total, block_sizes, listed):
    block_ends = jnp.cumsum(block_sizes)
    block_starts = block_ends - block_sizes
    positions = first_row + jnp.arange(row_total, dtype=jnp.int32)
    inside = (
        (positions[:, None] >= block_starts[None, :]) & (positions[:, None] < block_ends[None, :])
    ).astype(jnp.float32)
    return jnp.dot(
        inside,
        listed.astype(jnp.float32).T,
        precision=lax.Precision.HIGHEST,
        preferred_element_type=jnp.float32,
    )


def holder(k, n_rowdev, n_coldev):
    ratio = n_rowdev // n_coldev
    part = k // n_coldev
    place = k % n_coldev
    return (place + (part % 2) * (n_coldev - 1 - 2 * place)) * ratio + part


def shard_of(row, n_rowdev, n_coldev):
    ratio = n_rowdev // n_coldev
    part = row % ratio
    place = row // ratio
    return part * n_coldev + place + (part % 2) * (n_coldev - 1 - 2 * place)


def flip(row, bit):
    return row + bit * (1 - 2 * ((row // bit) % 2))


def product_kernel(
    n_rowdev, n_coldev, parts, depth,
    own_ref, inverse_ref, out_ref,
    panel, high, low, tiles, sums, from_below, from_above,
    gather_send, gather_recv, tile_sem, sum_send, below_recv, above_recv,
):
    row = lax.axis_index("row")
    col = lax.axis_index("col")
    sibling_count, shard_rows, width = own_ref.shape
    col_rows = panel.shape[1]
    piece = shard_rows // parts
    bits = [1 << i for i in range(n_rowdev.bit_length() - 1)]

    number = row * n_coldev + col
    target_row = holder(number % n_rowdev, n_rowdev, n_coldev)
    target_col = number // n_rowdev
    source = col * n_rowdev + shard_of(row, n_rowdev, n_coldev)
    source_row = source // n_coldev
    source_col = source % n_coldev
    moving = target_row * n_coldev + target_col != number

    barrier = pltpu.get_barrier_semaphore()

    def greet(to_row, to_col):
        pl.semaphore_signal(barrier, inc=1, device_id=(to_row, to_col), device_id_type=MESH)

    for bit in bits:
        greet(flip(row, bit), col)

    @pl.when(moving)
    def _():
        greet(target_row, target_col)
        greet(source_row, source_col)

    @pl.when(col > 0)
    def _():
        greet(row, col - 1)

    @pl.when(col < n_coldev - 1)
    def _():
        greet(row, col + 1)

    pl.semaphore_wait(
        barrier,
        len(bits)
        + jnp.where(moving, 2, 0)
        + jnp.where(col > 0, 1, 0)
        + jnp.where(col < n_coldev - 1, 1, 0),
    )

    def place(of_row, part):
        start = shard_of(of_row, n_rowdev, n_coldev) * shard_rows + part * piece
        return pl.ds(pl.multiple_of(start, 8), piece)

    def orders(part):
        rest = bits[1:]
        return (rest if part % 2 else rest[::-1]) + bits[:1]

    def move(s, part):
        return pltpu.make_async_remote_copy(
            src_ref=own_ref.at[s, pl.ds(part * piece, piece)],
            dst_ref=panel.at[s, place(target_row, part)],
            send_sem=gather_send.at[s, part, 0],
            recv_sem=gather_recv.at[s, part, 0],
            device_id=(target_row, target_col),
            device_id_type=MESH,
        )

    def keep(s, part):
        return pltpu.make_async_copy(
            own_ref.at[s, pl.ds(part * piece, piece)],
            panel.at[s, place(row, part)],
            gather_recv.at[s, part, 0],
        )

    def exchanges(s, part, stage):
        order = orders(part)
        held = [row]
        for bit in order[:stage - 1]:
            held = held + [flip(r, bit) for r in held]
        partner = flip(row, order[stage - 1])
        copies = []
        for m, slot in enumerate(held):
            entry = (1 << (stage - 1)) + m
            where = panel.at[s, place(slot, part)]
            copies.append(pltpu.make_async_remote_copy(
                src_ref=where,
                dst_ref=where,
                send_sem=gather_send.at[s, part, entry],
                recv_sem=gather_recv.at[s, part, entry],
                device_id=(partner, col),
                device_id_type=MESH,
            ))
        return copies

    def start_stage(s, part, stage):
        if stage == 0:
            @pl.when(moving)
            def _():
                move(s, part).start()

            @pl.when(jnp.logical_not(moving))
            def _():
                keep(s, part).start()
        else:
            for copy in exchanges(s, part, stage):
                copy.start()

    def end_stage(s, part, stage):
        if stage == 0:
            @pl.when(moving)
            def _():
                move(s, part).wait_recv()

            @pl.when(jnp.logical_not(moving))
            def _():
                keep(s, part).wait()
        else:
            for copy in exchanges(s, part, stage):
                copy.wait_recv()

    items = [(s, part) for s in range(sibling_count) for part in range(parts)]
    for s, part in items:
        start_stage(s, part, 0)

    others = (n_coldev - 1) * parts
    total = n_coldev * parts
    swap = col > n_coldev - 1 - col
    near = jnp.where(swap, n_coldev - 1 - col, col)
    lead = n_coldev - 1 - 2 * near
    minor_total = near * parts

    def plan(t):
        inner = t - lead
        paired = jnp.logical_and(inner >= 0, inner < 2 * minor_total)
        minor = jnp.logical_and(paired, inner % 2 == 1)
        major_at = jnp.where(inner < 0, t, jnp.where(paired, lead + inner // 2, t - minor_total))
        index = jnp.where(minor, inner // 2, major_at)
        up = jnp.where(swap, minor, jnp.logical_not(minor))
        block = jnp.where(up, n_coldev - 1 - index // parts, index // parts)
        is_own = t >= others
        block = jnp.where(is_own, col, block)
        part = jnp.where(is_own, t - others, index % parts)
        up = jnp.logical_and(up, jnp.logical_not(is_own))
        down = jnp.logical_and(jnp.logical_not(up), jnp.logical_not(is_own))
        return block, part, up, down, is_own

    def load(s, t):
        block, part, _, _, _ = plan(t % total)
        start = pl.multiple_of(block * shard_rows + part * piece, 8)
        slot = (s * total + t) % 2
        return pltpu.make_async_copy(
            inverse_ref.at[pl.ds(start, piece)], tiles.at[slot], tile_sem.at[slot]
        )

    load(0, 0).start()

    stages = 1 + len(bits)
    for tick in range(parts + stages):
        for part in range(parts):
            stage = tick - part
            if 0 <= stage < stages:
                end_stage(0, part, stage)
                if stage + 1 < stages:
                    start_stage(0, part, stage + 1)

    step = math.gcd(col_rows, 256)

    def split(s):
        @pl.loop(0, col_rows // step)
        def _(i):
            rows = pl.ds(pl.multiple_of(i * step, step), step)
            value = panel[s, rows, :]
            top = value.astype(jnp.bfloat16)
            high[s, rows, :] = top
            low[s, rows, :] = (value - top.astype(jnp.float32)).astype(jnp.bfloat16)

    def pass_up(s, block, part):
        return pltpu.make_async_remote_copy(
            src_ref=sums.at[s, block, part],
            dst_ref=from_below.at[s, block, part],
            send_sem=sum_send.at[s, block, part],
            recv_sem=below_recv.at[s, block, part],
            device_id=(row, col + 1),
            device_id_type=MESH,
        )

    def pass_down(s, block, part):
        return pltpu.make_async_remote_copy(
            src_ref=sums.at[s, block, part],
            dst_ref=from_above.at[s, block, part],
            send_sem=sum_send.at[s, block, part],
            recv_sem=above_recv.at[s, block, part],
            device_id=(row, col - 1),
            device_id_type=MESH,
        )

    hooks = [(stage, part) for stage in range(stages - 1) for part in range(parts)]

    def advance(s, hook):
        stage, part = hook
        end_stage(s, part, stage)
        start_stage(s, part, stage + 1)

    for s in range(sibling_count):
        split(s)
        follows = s + 1 < sibling_count

        @pl.loop(0, total)
        def _(t):
            block, part, up, down, is_own = plan(t)
            slot = (s * total + t) % 2

            @pl.when(t + 1 < (total + 1 if follows else total))
            def _():
                load(s, t + 1).start()

            load(s, t).wait()
            sums[s, block, part] = jnp.zeros((piece, width), jnp.float32)

            @pl.loop(0, col_rows // depth)
            def _(k):
                span = pl.ds(pl.multiple_of(k * depth, depth), depth)
                value = tiles[slot, :, span]
                top = value.astype(jnp.bfloat16)
                rest = (value - top.astype(jnp.float32)).astype(jnp.bfloat16)
                dot = functools.partial(jnp.dot, preferred_element_type=jnp.float32)
                sums[s, block, part] += (
                    dot(top, low[s, span, :])
                    + dot(rest, high[s, span, :])
                    + dot(top, high[s, span, :])
                )

            @pl.when(jnp.logical_and(jnp.logical_not(down), col > 0))
            def _():
                pass_up(s, block, part).wait_recv()
                sums[s, block, part] += from_below[s, block, part]

            @pl.when(jnp.logical_and(jnp.logical_not(up), col < n_coldev - 1))
            def _():
                pass_down(s, block, part).wait_recv()
                sums[s, block, part] += from_above[s, block, part]

            @pl.when(up)
            def _():
                pass_up(s, block, part).start()

            @pl.when(down)
            def _():
                pass_down(s, block, part).start()

            @pl.when(is_own)
            def _():
                out_ref[s, part] = sums[s, block, part]

            if follows:
                for at, hook in enumerate(hooks[:total]):
                    @pl.when(t == at)
                    def _(hook=hook):
                        advance(s + 1, hook)

        if follows:
            for hook in hooks[total:]:
                advance(s + 1, hook)
            for part in range(parts):
                end_stage(s + 1, part, stages - 1)

    for s in range(sibling_count):
        @pl.loop(0, others)
        def _(t):
            block, part, up, down, _ = plan(t)

            @pl.when(up)
            def _():
                pass_up(s, block, part).wait_send()

            @pl.when(down)
            def _():
                pass_down(s, block, part).wait_send()

    for s, part in items:
        @pl.when(moving)
        def _():
            move(s, part).wait_send()

        for stage in range(1, stages):
            for copy in exchanges(s, part, stage):
                copy.wait_send()


def product(n_rowdev, n_coldev, inverse, own):
    sibling_count, shard_rows, width = own.shape
    block_total, col_rows = inverse.shape
    parts = 2 if shard_rows % 16 == 0 else 1
    piece = shard_rows // parts
    depth = math.gcd(col_rows, 1280)
    f32 = jnp.float32
    vmem = pl.BlockSpec(memory_space=pltpu.VMEM)
    out = pl.pallas_call(
        functools.partial(product_kernel, n_rowdev, n_coldev, parts, depth),
        out_shape=jax.ShapeDtypeStruct((sibling_count, parts, piece, width), f32),
        in_specs=[vmem, pl.BlockSpec(memory_space=pl.ANY)],
        out_specs=vmem,
        scratch_shapes=[
            pltpu.VMEM((sibling_count, col_rows, width), f32),
            pltpu.VMEM((sibling_count, col_rows, width), jnp.bfloat16),
            pltpu.VMEM((sibling_count, col_rows, width), jnp.bfloat16),
            pltpu.VMEM((2, piece, col_rows), f32),
            pltpu.VMEM((sibling_count, n_coldev, parts, piece, width), f32),
            pltpu.VMEM((sibling_count, n_coldev, parts, piece, width), f32),
            pltpu.VMEM((sibling_count, n_coldev, parts, piece, width), f32),
            pltpu.SemaphoreType.DMA((sibling_count, parts, n_rowdev)),
            pltpu.SemaphoreType.DMA((sibling_count, parts, n_rowdev)),
            pltpu.SemaphoreType.DMA((2,)),
            pltpu.SemaphoreType.DMA((sibling_count, n_coldev, parts)),
            pltpu.SemaphoreType.DMA((sibling_count, n_coldev, parts)),
            pltpu.SemaphoreType.DMA((sibling_count, n_coldev, parts)),
        ],
        compiler_params=pltpu.CompilerParams(
            collective_id=0, has_side_effects=True, vmem_limit_bytes=60_000_000
        ),
        name="gather_product_scatter",
    )(own, inverse)
    return out.reshape(sibling_count, shard_rows, width)


def total_kernel(
    n_rowdev, n_coldev, x_ref, out_ref,
    got, mine, gathered, whole, first_send, first_recv, second_send, second_recv,
    third_send, third_recv,
):
    row = lax.axis_index("row")
    col = lax.axis_index("col")
    barrier = pltpu.get_barrier_semaphore()
    for step in range(1, n_rowdev):
        pl.semaphore_signal(
            barrier, inc=1, device_id=((row + step) % n_rowdev, col), device_id_type=MESH
        )
    for step in range(1, n_coldev):
        pl.semaphore_signal(
            barrier, inc=1, device_id=(row, (col + step) % n_coldev), device_id_type=MESH
        )
    pl.semaphore_wait(barrier, n_rowdev + n_coldev - 2)

    def scatter(step):
        peer = (row + step) % n_rowdev
        return pltpu.make_async_remote_copy(
            src_ref=x_ref.at[peer], dst_ref=got.at[step],
            send_sem=first_send.at[step], recv_sem=first_recv.at[step],
            device_id=(peer, col), device_id_type=MESH,
        )

    def share(step):
        return pltpu.make_async_remote_copy(
            src_ref=mine, dst_ref=gathered.at[step],
            send_sem=second_send.at[step], recv_sem=second_recv.at[step],
            device_id=(row, (col + step) % n_coldev), device_id_type=MESH,
        )

    def spread(step):
        return pltpu.make_async_remote_copy(
            src_ref=whole, dst_ref=out_ref.at[row],
            send_sem=third_send.at[step], recv_sem=third_recv.at[step],
            device_id=((row + step) % n_rowdev, col), device_id_type=MESH,
        )

    for step in range(1, n_rowdev):
        scatter(step).start()
    value = x_ref[row]
    for step in range(1, n_rowdev):
        scatter(step).wait_recv()
        value = value + got[step]
    mine[...] = value
    for step in range(1, n_coldev):
        share(step).start()
    for step in range(1, n_coldev):
        share(step).wait_recv()
    gathered[0] = mine[...]
    value = gathered[col]
    for place in range(1, n_coldev):
        value = value + gathered[(col - place + n_coldev) % n_coldev]
    whole[...] = value
    for step in range(1, n_rowdev):
        spread(step).start()
    out_ref[row] = whole[...]
    for step in range(1, n_rowdev):
        spread(step).wait_recv()
    for step in range(1, n_rowdev):
        scatter(step).wait_send()
        spread(step).wait_send()
    for step in range(1, n_coldev):
        share(step).wait_send()


def total(n_rowdev, n_coldev, value):
    rows, columns = value.shape
    piece = rows // n_rowdev
    vmem = pl.BlockSpec(memory_space=pltpu.VMEM)
    dma = pltpu.SemaphoreType.DMA
    out = pl.pallas_call(
        functools.partial(total_kernel, n_rowdev, n_coldev),
        out_shape=jax.ShapeDtypeStruct((n_rowdev, piece, columns), jnp.float32),
        in_specs=[vmem],
        out_specs=vmem,
        scratch_shapes=[
            pltpu.VMEM((n_rowdev, piece, columns), jnp.float32),
            pltpu.VMEM((piece, columns), jnp.float32),
            pltpu.VMEM((n_coldev, piece, columns), jnp.float32),
            pltpu.VMEM((piece, columns), jnp.float32),
            dma((n_rowdev,)), dma((n_rowdev,)), dma((n_coldev,)), dma((n_coldev,)),
            dma((n_rowdev,)), dma((n_rowdev,)),
        ],
        compiler_params=pltpu.CompilerParams(collective_id=1, has_side_effects=True),
        name="schur_total",
    )(value.reshape(n_rowdev, piece, columns))
    return out.reshape(rows, columns)


def per_device(inverse, factor, diag_inverse, block_sizes, listed):
    n_rowdev = lax.axis_size("row")
    n_coldev = lax.axis_size("col")
    row_place = lax.axis_index("row")
    col_place = lax.axis_index("col")
    shard_rows, sibling_count, width = factor.shape

    member = membership(
        (row_place * n_coldev + col_place) * shard_rows, shard_rows, block_sizes, listed
    )
    own = jnp.transpose(factor, (1, 0, 2))
    summed = product(n_rowdev, n_coldev, inverse, own * member.T[:, :, None])
    results = [
        -(summed[s] * member[:, s:s + 1])
        for s in range(sibling_count)
    ]
    terms = [
        lax.dot_general(
            own[s], results[s], (((0,), (0,)), ((), ())),
            precision=lax.Precision.HIGHEST, preferred_element_type=jnp.float32,
        )
        for s in range(sibling_count)
    ]
    schur = total(n_rowdev, n_coldev, jnp.concatenate(terms, axis=0))
    schur = schur.reshape(sibling_count, width, width)
    ancestor_rows = jnp.stack(results, axis=1)
    return (ancestor_rows, diag_inverse - schur)


def solution(mesh):
    in_specs = (P("row", "col"), P(("row", "col"), None, None), P(), P(), P())
    out_specs = (P(("row", "col"), None, None), P())
    return jax.shard_map(
        per_device, mesh=mesh, in_specs=in_specs, out_specs=out_specs, check_vma=False
    )
```
